32 devices in a mesh: shots: 2 (over y), wide: 16 (over z, x, core).
Axes of the slice: x: 2, y: 2, z: 4, core: 2. Of those that a mesh axis runs over, the one named last changes fastest.
Arguments:
- src_now: float32 [32, 64, 128], P('wide', 'shots'), parts along dimension 1, may hold values from -6 to 6
- src_old: float32 [32, 64, 128], P('wide', 'shots'), parts along dimension 1, may hold values from -6 to 6
- rcv_now: float32 [32, 256, 32], P('wide', 'shots'), parts along dimension 1, may hold values from -6 to 6
- rcv_old: float32 [32, 256, 32], P('wide', 'shots'), parts along dimension 1, may hold values from -6 to 6
- medium: float32 [3, 32, 128, 32], P(None, 'wide'), may hold values from 0.04 to 0.24
- wavelet: float32 [4], replicated, may hold values from -4 to 4
- shot: int32 [6], P('shots'), parts along dimension 0, may hold values from 0 to 31
- traces: float32 [32, 128, 4], P('wide', 'shots'), parts along dimension 1, may hold values from -6 to 6
- rec_x: int32 [32, 128], P('wide', 'shots'), parts along dimension 1, may hold values from 0 to 31
- lag_order: int32 [33], replicated, may hold values from 0 to 32, each once
Outputs:
- src_next: float32 [32, 64, 128], P('wide', 'shots'), parts along dimension 1
- src_prior: float32 [32, 64, 128], P('wide', 'shots'), parts along dimension 1
- rcv_next: float32 [32, 256, 32], P('wide', 'shots'), parts along dimension 1
- rcv_prior: float32 [32, 256, 32], P('wide', 'shots'), parts along dimension 1
- image: float32 [66, 32, 128, 32], P('shots', 'wide'), parts along dimension 0
The draws below stay inside these ranges and needn't reach their ends.
There are 2 independent parts, one for each index of `shots`. The reference program is written for one: setup_inputs(seed, part) draws one part's arguments, and reference() takes and returns one part's arrays. A program takes and returns all parts, laid end to end along the dimension named above; an argument that names none is the same for every part. Nothing has to cross between parts.
Inputs may be any that keep to these rules, and one draw needn't show every extreme that they name: `lag_order`: each of the 33 lag slots once.
All inputs are finite; a program needn't handle non-finite values.
Results may differ from the reference program's by a relative error of at most 0.0003.
Values sent between devices are 32-bit elements; how exact they have to be, the bound alone decides.
A program may use at most 64 MiB of HBM per device.

```python
import math
import jax
import jax.numpy as jnp
from jax import lax

Z = 128
RX = 64
STEPS = 4
LAGS = 33
X = 32
Y = 32


def place_ends(values, key, smallest, high):
    extent = values.shape
    spot = [jax.random.randint(jax.random.fold_in(key, axis), (), 0, extent[axis]) for axis in range(len(extent))]
    values = values.at[tuple(spot)].set(smallest)
    longest = extent.index(max(extent))
    spot[longest] = (spot[longest] + 1) % extent[longest]
    return values.at[tuple(spot)].set(high)


def shard_levels(own_key, extent, cuts, low, high):
    def one(axis_at, shards_of):
        steps = jax.random.uniform(jax.random.fold_in(jax.random.fold_in(own_key, 6), axis_at), (shards_of,), jnp.float32, low / len(cuts), high / len(cuts))
        return jnp.repeat(jnp.exp(steps), extent[axis_at] // shards_of).reshape((-1,) + (1,) * (len(extent) - axis_at - 1))

    gain = one(*cuts[0])
    for cut in cuts[1:]:
        gain = gain * one(*cut)
    return gain


def normal_values(key, extent, scale, reach, split=(), kind=jnp.bfloat16):
    entries = scale * jax.random.normal(key, extent, jnp.float32)
    if split:
        entries = entries * shard_levels(key, extent, split, -0.22, 0.18)
    return jnp.clip(entries, -reach, reach).astype(kind)


def setup_inputs(seed: int = 0, part: int = 0) -> dict:
    key_of = jax.random.split(jax.random.key(seed), 11)
    part_keys = jax.random.split(jax.random.fold_in(key_of[10], part), 11)
    return {
        "src_now": normal_values(part_keys[0], (X, Y, Z), 1.0, 6.0, ((0, 16),), jnp.float32),
        "src_old": normal_values(part_keys[1], (X, Y, Z), 1.0, 6.0, ((0, 16),), jnp.float32),
        "rcv_now": normal_values(part_keys[2], (Y, Z, X), 1.0, 6.0, ((0, 16),), jnp.float32),
        "rcv_old": normal_values(part_keys[3], (Y, Z, X), 1.0, 6.0, ((0, 16),), jnp.float32),
        "medium": jnp.clip(jnp.exp(math.log(0.24) - 1.7917595 * jax.random.uniform(key_of[4], (3, Y, Z, X), jnp.float32) ** shard_levels(key_of[4], (3, Y, Z, X), ((1, 16),), -0.2, 0.2)), 0.04, 0.24),
        "wavelet": normal_values(key_of[5], (STEPS,), 1.0, 4.0, (), jnp.float32),
        "shot": jax.random.randint(part_keys[6], (3,), 0, min(X, Y, Z)).astype(jnp.int32),
        "traces": normal_values(part_keys[7], (Y, RX, STEPS), 1.0, 6.0, ((0, 16),), jnp.float32),
        "rec_x": place_ends(jax.random.randint(part_keys[8], (Y, RX), 0, X), jax.random.fold_in(part_keys[8], 1), 0, X - 1).astype(jnp.int32),
        "lag_order": jax.random.permutation(key_of[9], LAGS).astype(jnp.int32),
    }


def window_sum(padded, dim, count):
    def window_at(start):
        return lax.slice_in_dim(padded, start, start + count, axis=dim)
    return (-1.0 / 12.0) * (window_at(0) + window_at(4)) + (4.0 / 3.0) * (window_at(1) + window_at(3)) - 2.5 * window_at(2)


def widen(field, dim):
    widths = [(0, 0)] * field.ndim
    widths[dim] = (2, 2)
    return jnp.pad(field, widths)


def second(field, dim):
    return window_sum(widen(field, dim), dim, field.shape[dim])


def lagged(snaps, lag_order):
    half = (lag_order.shape[0] - 1) // 2
    cells_x = snaps[0][0].shape[2]
    widths = ((0, 0), (0, 0), (half, half))
    padded = [(jnp.pad(source, widths), jnp.pad(receiver, widths)) for source, receiver in snaps]

    def one_plane(slot):
        offset = slot.astype(jnp.int32) - half
        total = None
        for source, receiver in padded:
            moved_src = lax.dynamic_slice_in_dim(source, (half - offset).astype(jnp.int32), cells_x, 2)
            moved_rcv = lax.dynamic_slice_in_dim(receiver, (half + offset).astype(jnp.int32), cells_x, 2)
            product = moved_src * moved_rcv
            total = product if total is None else total + product
        return total

    return lax.map(one_plane, lag_order)


def reference(src_now, src_old, rcv_now, rcv_old, medium, wavelet, shot, traces, rec_x, lag_order):
    cells_x, cells_y, cells_z = src_now.shape
    src_speed = jnp.transpose(medium, (0, 3, 1, 2))
    shot_cell = ((jnp.arange(cells_x, dtype=jnp.int32) == shot[0]).astype(jnp.float32)[:, None, None]
                 * (jnp.arange(cells_y, dtype=jnp.int32) == shot[1]).astype(jnp.float32)[None, :, None]
                 * (jnp.arange(cells_z, dtype=jnp.int32) == shot[2]).astype(jnp.float32)[None, None, :])
    onehot = (rec_x[:, :, None] == jnp.arange(cells_x, dtype=jnp.int32)[None, None, :]).astype(jnp.float32)
    snaps = []
    for step in range(wavelet.shape[0]):
        spread = src_speed[0] * second(src_now, 0) + src_speed[1] * second(src_now, 1) + src_speed[2] * second(src_now, 2)
        src_new = 2.0 * src_now - src_old + spread - wavelet[step] * shot_cell
        spread_rcv = medium[0] * second(rcv_now, 2) + medium[1] * second(rcv_now, 0) + medium[2] * second(rcv_now, 1)
        rcv_new = 2.0 * rcv_now - rcv_old + spread_rcv
        surface = jnp.einsum("yr,yrx->yx", traces[:, :, step], onehot, precision=lax.Precision.HIGHEST)
        rcv_new = rcv_new.at[:, 0, :].add(surface)
        src_old, src_now = src_now, src_new
        rcv_old, rcv_now = rcv_now, rcv_new
        if step % 2 == 1:
            snaps.append((jnp.transpose(src_now, (1, 2, 0)), rcv_now))
    image = lagged(snaps, lag_order)
    return src_now, src_old, rcv_now, rcv_old, image
```

```python
import functools

import jax
import jax.numpy as jnp
from jax import lax
from jax.experimental import pallas as pl
from jax.experimental.pallas import tpu as pltpu
from jax.sharding import PartitionSpec as P

REACH = 2
EDGE = 8
OUTER, INNER, CENTRE = -1.0 / 12.0, 4.0 / 3.0, -2.5
SRC, RCV = 0, 1


def second(window):
    return (
        OUTER * (window(-2) + window(2)) + INNER * (window(-1) + window(1)) + CENTRE * window(0)
    )


def window_kernel(
    devices,
    src_now,
    src_old,
    rcv_now,
    rcv_old,
    medium,
    wavelet,
    shot,
    traces,
    rec_x,
    src_next,
    src_prior,
    rcv_next,
    rcv_prior,
    snaps,
    staged,
    landed,
    levels,
    partial,
    surface,
    spot,
    leaving,
    returned,
    out_send,
    out_recv,
    back_send,
    back_recv,
    halo_send,
    halo_recv,
):
    me = lax.axis_index("wide")
    slab_x, cells_y, cells_z = src_now.shape
    slab_y, cells_x, _ = rcv_now.shape
    steps = wavelet.shape[0]
    span = slab_y + 2 * REACH
    rows = staged.shape[0] // (devices * slab_x)
    block = slab_x * rows
    back_rows = 2 * slab_x * slab_y
    inside = pl.ds(EDGE, cells_x)

    barrier = pltpu.get_barrier_semaphore()

    @pl.loop(1, devices)
    def _(distance):
        pl.semaphore_signal(
            barrier,
            inc=1,
            device_id={"wide": lax.rem(me + distance, devices)},
            device_id_type=MESH,
        )

    for peer in range(devices):
        first = peer * slab_y - REACH
        low, high = max(first, 0), min(first + span, cells_y)
        for x in range(slab_x):
            base = (peer * slab_x + x) * rows
            if low > first or high < first + span:
                staged[base : base + rows, :] = jnp.zeros((rows, cells_z), jnp.float32)
            staged[base + low - first : base + high - first, :] = src_now[x, low:high, :]
            staged[base + span : base + span + slab_y, :] = src_old[
                x, peer * slab_y : (peer + 1) * slab_y, :
            ]

    zero_edge = jnp.zeros((EDGE, cells_z), jnp.float32)
    zero_plane = jnp.zeros((cells_x, cells_z), jnp.float32)
    for level in range(steps):
        for field in (SRC, RCV):
            for y in range(REACH, REACH + slab_y):
                levels[level, field, y, 0:EDGE, :] = zero_edge
                levels[level, field, y, EDGE + cells_x : EDGE + cells_x + EDGE, :] = zero_edge

    @pl.when(me == 0)
    def _():
        for level in range(steps):
            for field in (SRC, RCV):
                for y in range(REACH):
                    levels[level, field, y, inside, :] = zero_plane

    @pl.when(me == devices - 1)
    def _():
        for level in range(steps):
            for field in (SRC, RCV):
                for y in range(REACH):
                    levels[level, field, REACH + slab_y + y, inside, :] = zero_plane

    for y in range(slab_y):
        levels[0, RCV, REACH + y, inside, :] = rcv_now[y]

    pl.semaphore_wait(barrier, devices - 1)

    def out_copy(peer):
        return pltpu.make_async_remote_copy(
            src_ref=staged.at[pl.ds(pl.multiple_of(peer * block, 8), block)],
            dst_ref=landed.at[pl.ds(pl.multiple_of(me * block, 8), block)],
            send_sem=out_send,
            recv_sem=out_recv,
            device_id={"wide": peer},
            device_id_type=MESH,
        )

    def halo_copy(field, level, side):
        if level == 0:
            first = slab_y - REACH if side == 0 else 0
            source = rcv_now.at[pl.ds(first, REACH)]
        else:
            first = slab_y if side == 0 else REACH
            source = levels.at[level, field, pl.ds(first, REACH), inside]
        into = 0 if side == 0 else REACH + slab_y
        peer = me + 1 if side == 0 else me - 1
        return pltpu.make_async_remote_copy(
            src_ref=source,
            dst_ref=levels.at[level, field, pl.ds(into, REACH), inside],
            send_sem=halo_send.at[field, level, side],
            recv_sem=halo_recv.at[field, level, side],
            device_id={"wide": peer},
            device_id_type=MESH,
        )

    def each_side(field, level, act):
        @pl.when(me < devices - 1)
        def _():
            act(0)

        @pl.when(me > 0)
        def _():
            act(1)

    def send_halo(field, level):
        each_side(field, level, lambda side: halo_copy(field, level, side).start())

    def wait_halo(field, level):
        each_side(field, level, lambda side: halo_copy(field, level, 1 - side).wait_recv())

    def wait_sent(field, level):
        each_side(field, level, lambda side: halo_copy(field, level, side).wait_send())

    @pl.loop(1, devices)
    def _(distance):
        out_copy(lax.rem(me + distance, devices)).start()

    send_halo(RCV, 0)

    own = pl.ds(pl.multiple_of(me * block, 8), block)
    landed[own, :] = staged[own, :]

    row_at = lax.broadcasted_iota(jnp.int32, (cells_x, cells_z), 0)
    lane_at = lax.broadcasted_iota(jnp.int32, (cells_x, cells_z), 1)
    column = ((row_at == shot[0]) & (lane_at == shot[2])).astype(jnp.float32)
    for y in range(slab_y):
        spot[y] = column * (me * slab_y + y == shot[1]).astype(jnp.float32)
    x_at = lax.broadcasted_iota(jnp.int32, (cells_x, traces.shape[2]), 0)
    for y in range(slab_y):
        onehot = (x_at == rec_x[y : y + 1, :]).astype(jnp.float32)
        for step in range(steps):
            total = jnp.sum(onehot * traces[y, step : step + 1, :], axis=1, keepdims=True)
            surface[step, y] = jnp.where(lane_at == 0, total, 0.0)

    def older(field, level, y):
        if level > 0:
            return levels[level - 1, field, REACH + y, inside, :]
        if field == RCV:
            return rcv_old[y]
        return landed[pl.ds(span + y, cells_x, stride=rows), :]

    def local(field, level):
        for y in range(slab_y):
            centre = levels[level, field, REACH + y, inside, :]

            def along_x(shift):
                if shift == 0:
                    return centre
                return levels[level, field, REACH + y, pl.ds(EDGE + shift, cells_x), :]

            def along_z(shift):
                if shift == 0:
                    return centre
                turned = pltpu.roll(centre, (-shift) % cells_z, 1)
                kept = lane_at >= -shift if shift < 0 else lane_at < cells_z - shift
                return jnp.where(kept, turned, 0.0)

            partial[field, y] = (
                2.0 * centre
                - older(field, level, y)
                + medium[0, y] * second(along_x)
                + medium[2, y] * second(along_z)
            )

    def finish(field, level):
        for y in range(slab_y):
            def along_y(shift):
                return levels[level, field, REACH + y + shift, inside, :]

            if field == SRC:
                added = -wavelet[level] * spot[y]
            else:
                added = surface[level, y]
            levels[level + 1, field, REACH + y, inside, :] = (
                partial[field, y] + medium[1, y] * second(along_y) + added
            )

    local(RCV, 0)
    wait_halo(RCV, 0)
    finish(RCV, 0)
    send_halo(RCV, 1)
    local(RCV, 1)

    arrived = landed.at[pl.ds(0, (devices - 1) * block)]
    pltpu.make_async_copy(arrived, arrived, out_recv).wait()
    for y in range(span):
        levels[0, SRC, y, inside, :] = landed[pl.ds(y, cells_x, stride=rows), :]
    local(SRC, 0)
    finish(SRC, 0)
    for level in range(1, steps):
        send_halo(SRC, level)
        local(SRC, level)
        wait_halo(RCV, level)
        finish(RCV, level)
        if level + 1 < steps:
            send_halo(RCV, level + 1)
            local(RCV, level + 1)
        wait_halo(SRC, level)
        finish(SRC, level)

    for back, level in enumerate((steps, steps - 1)):
        for x in range(slab_x):
            for y in range(slab_y):
                at = (back * slab_x + x) * slab_y + y
                leaving[pl.ds(at, devices, stride=back_rows), :] = levels[
                    level, SRC, REACH + y, pl.ds(EDGE + x, devices, stride=slab_x), :
                ]

    def back_copy(peer):
        return pltpu.make_async_remote_copy(
            src_ref=leaving.at[pl.ds(pl.multiple_of(peer * back_rows, 8), back_rows)],
            dst_ref=returned.at[pl.ds(pl.multiple_of(me * back_rows, 8), back_rows)],
            send_sem=back_send,
            recv_sem=back_recv,
            device_id={"wide": peer},
            device_id_type=MESH,
        )

    @pl.loop(1, devices)
    def _(distance):
        back_copy(lax.rem(me + distance, devices)).start()

    own_back = pl.ds(pl.multiple_of(me * back_rows, 8), back_rows)
    returned[own_back, :] = leaving[own_back, :]
    for y in range(slab_y):
        rcv_next[y] = levels[steps, RCV, REACH + y, inside, :]
        rcv_prior[y] = levels[steps - 1, RCV, REACH + y, inside, :]
        for field in (SRC, RCV):
            for snap in range(snaps.shape[0]):
                snaps[snap, field, y] = levels[2 * snap + 2, field, REACH + y, inside, :]

    sent = staged.at[pl.ds(0, (devices - 1) * block)]
    pltpu.make_async_copy(sent, sent, out_send).wait()
    for level in range(steps):
        wait_sent(RCV, level)
        if level > 0:
            wait_sent(SRC, level)

    came = returned.at[pl.ds(0, (devices - 1) * back_rows)]
    pltpu.make_async_copy(came, came, back_recv).wait()
    for back, result in enumerate((src_next, src_prior)):
        for x in range(slab_x):
            for y in range(slab_y):
                at = (back * slab_x + x) * slab_y + y
                result[x, pl.ds(y, devices, stride=slab_y), :] = returned[
                    pl.ds(at, devices, stride=back_rows), :
                ]
    gone = leaving.at[pl.ds(0, (devices - 1) * back_rows)]
    pltpu.make_async_copy(gone, gone, back_send).wait()


def image_kernel(lag_order, snaps, a, b, c, d, a_out, b_out, c_out, d_out, image, padded, board, sems):
    lags = lag_order.shape[0]
    half = (lags - 1) // 2
    taken, fields, slab_y, cells_x, cells_z = snaps.shape
    edge = jnp.zeros((half, cells_z), jnp.float32)
    for snap in range(taken):
        for field in range(fields):
            for y in range(slab_y):
                padded[snap, field, y, 0:half, :] = edge
                padded[snap, field, y, half : half + cells_x, :] = snaps[snap, field, y]
                padded[snap, field, y, half + cells_x : 2 * half + cells_x, :] = edge
    chunk = -(-lags // 3)
    copies = []
    for part, first in enumerate(range(0, lags, chunk)):
        count = min(chunk, lags - first)
        for plane in range(first, first + count):
            slot = lag_order[plane]
            at_src = pl.ds(2 * half - slot, cells_x)
            at_rcv = pl.ds(slot, cells_x)
            for y in range(slab_y):
                total = None
                for snap in range(taken):
                    product = padded[snap, SRC, y, at_src, :] * padded[snap, RCV, y, at_rcv, :]
                    total = product if total is None else total + product
                board[plane, y] = total
        copy = pltpu.make_async_copy(
            board.at[pl.ds(first, count)], image.at[pl.ds(first, count)], sems.at[part]
        )
        copy.start()
        copies.append(copy)
    a_out[...] = a[...]
    b_out[...] = b[...]
    c_out[...] = c[...]
    d_out[...] = d[...]
    for copy in copies:
        copy.wait()


MESH = pl.DeviceIdType.MESH


def solution(mesh):
    devices = mesh.shape["wide"]

    def on_device(
        src_now, src_old, rcv_now, rcv_old, medium, wavelet, shot, traces, rec_x, lag_order
    ):
        slab_x, cells_y, cells_z = src_now.shape
        slab_y, _, cells_x = rcv_now.shape
        steps = wavelet.shape[0]
        lags = lag_order.shape[0]
        half = (lags - 1) // 2
        span = slab_y + 2 * REACH
        rows = -(-(span + slab_y) // 8) * 8
        f32 = jnp.float32
        vmem = pl.BlockSpec(memory_space=pltpu.VMEM)
        smem = pl.BlockSpec(memory_space=pltpu.SMEM)
        src_shape = jax.ShapeDtypeStruct((slab_x, cells_y, cells_z), f32)
        rcv_shape = jax.ShapeDtypeStruct((slab_y, cells_x, cells_z), f32)
        taken = steps // 2
        turn = lambda array: jnp.swapaxes(array, -1, -2)
        src_next, src_prior, rcv_next, rcv_prior, snaps = pl.pallas_call(
            functools.partial(window_kernel, devices),
            out_shape=(
                src_shape,
                src_shape,
                rcv_shape,
                rcv_shape,
                jax.ShapeDtypeStruct((taken, 2, slab_y, cells_x, cells_z), f32),
            ),
            in_specs=[vmem] * 5 + [smem] * 2 + [vmem] * 2,
            out_specs=(vmem,) * 5,
            scratch_shapes=[
                pltpu.VMEM((cells_x * rows, cells_z), f32),
                pltpu.VMEM((cells_x * rows, cells_z), f32),
                pltpu.VMEM((steps + 1, 2, span, cells_x + 2 * EDGE, cells_z), f32),
                pltpu.VMEM((2, slab_y, cells_x, cells_z), f32),
                pltpu.VMEM((steps, slab_y, cells_x, cells_z), f32),
                pltpu.VMEM((slab_y, cells_x, cells_z), f32),
                pltpu.VMEM((devices * 2 * slab_x * slab_y, cells_z), f32),
                pltpu.VMEM((devices * 2 * slab_x * slab_y, cells_z), f32),
                pltpu.SemaphoreType.DMA,
                pltpu.SemaphoreType.DMA,
                pltpu.SemaphoreType.DMA,
                pltpu.SemaphoreType.DMA,
                pltpu.SemaphoreType.DMA((2, steps, 2)),
                pltpu.SemaphoreType.DMA((2, steps, 2)),
            ],
            compiler_params=pltpu.CompilerParams(collective_id=0, has_side_effects=True),
            name="window",
        )(
            src_now,
            src_old,
            turn(rcv_now),
            turn(rcv_old),
            turn(medium),
            wavelet,
            shot,
            turn(traces),
            rec_x,
        )
        outs = pl.pallas_call(
            image_kernel,
            out_shape=(
                src_shape,
                src_shape,
                rcv_shape,
                rcv_shape,
                jax.ShapeDtypeStruct((lags, slab_y, cells_x, cells_z), f32),
            ),
            in_specs=[smem] + [vmem] * 5,
            out_specs=(vmem,) * 4 + (pl.BlockSpec(memory_space=pl.ANY),),
            scratch_shapes=[
                pltpu.VMEM((taken, 2, slab_y, cells_x + 2 * half, cells_z), f32),
                pltpu.VMEM((lags, slab_y, cells_x, cells_z), f32),
                pltpu.SemaphoreType.DMA((3,)),
            ],
            name="image",
        )(lag_order, snaps, src_next, src_prior, rcv_next, rcv_prior)
        return outs[0], outs[1], turn(outs[2]), turn(outs[3]), turn(outs[4])

    return jax.shard_map(
        on_device,
        mesh=mesh,
        in_specs=(
            P("wide", "shots", None),
            P("wide", "shots", None),
            P("wide", "shots", None),
            P("wide", "shots", None),
            P(None, "wide", None, None),
            P(),
            P("shots"),
            P("wide", "shots", None),
            P("wide", "shots"),
            P(),
        ),
        out_specs=(
            P("wide", "shots", None),
            P("wide", "shots", None),
            P("wide", "shots", None),
            P("wide", "shots", None),
            P("shots", "wide", None, None),
        ),
        check_vma=False,
    )
```

```python
import functools
import math

import jax
import jax.numpy as jnp
from jax import lax
from jax.experimental import pallas as pl
from jax.experimental.pallas import tpu as pltpu
from jax.sharding import PartitionSpec as P

REACH = 2
EDGE = 8
OUTER, INNER, CENTRE = -1.0 / 12.0, 4.0 / 3.0, -2.5
SRC, RCV = 0, 1


def second(window):
    return (
        OUTER * (window(-2) + window(2)) + INNER * (window(-1) + window(1)) + CENTRE * window(0)
    )


def window_kernel(
    devices,
    src_now_in,
    src_old_in,
    rcv_now_in,
    rcv_old_in,
    medium_in,
    wavelet_in,
    shot_in,
    traces_in,
    rec_x_in,
    lag_order_in,
    src_next,
    src_prior,
    rcv_next,
    rcv_prior,
    board,
    src_now,
    src_old,
    rcv_old,
    medium,
    wavelet,
    shot,
    traces,
    rec_x,
    lag_order,
    padded,
    staged,
    landed,
    levels,
    partial,
    surface,
    spot,
    leaving,
    returned,
    out_send,
    out_recv,
    back_send,
    back_recv,
    halo_send,
    halo_recv,
    load_sems,
):
    me = lax.axis_index("wide")
    slab_x, cells_y, cells_z = src_now.shape
    slab_y, cells_x, _ = rcv_old.shape
    steps = wavelet.shape[0]
    span = slab_y + 2 * REACH
    rows = staged.shape[0] // (devices * slab_x)
    block = slab_x * rows
    back_rows = 2 * slab_x * slab_y
    inside = pl.ds(EDGE, cells_x)

    lags = lag_order.shape[0]
    half = (lags - 1) // 2
    middle = devices // 2
    far_first = sorted(range(1, devices), key=lambda distance: abs(distance - middle))

    loads = []
    for index, (source, target) in enumerate(
        (
            (src_now_in, src_now),
            (src_old_in, src_old),
            (rcv_now_in, levels.at[0, RCV, pl.ds(REACH, slab_y), inside]),
            (shot_in, shot),
            (traces_in, traces),
            (rec_x_in, rec_x),
            (rcv_old_in, rcv_old),
            (medium_in, medium),
            (wavelet_in, wavelet),
            (lag_order_in, lag_order),
        )
    ):
        loads.append(pltpu.make_async_copy(source, target, load_sems.at[index]))
    for load in loads[:3]:
        load.start()

    barrier = pltpu.get_barrier_semaphore()
    for distance in far_first:
        pl.semaphore_signal(
            barrier,
            inc=1,
            device_id={"wide": lax.rem(me + distance, devices)},
            device_id_type=MESH,
        )
    for load in loads[3:]:
        load.start()

    zero_edge = jnp.zeros((EDGE, cells_z), jnp.float32)
    zero_plane = jnp.zeros((cells_x, cells_z), jnp.float32)
    zero_half = jnp.zeros((half, cells_z), jnp.float32)
    for snap in range(padded.shape[0]):
        for field in (SRC, RCV):
            for y in range(slab_y):
                padded[snap, field, y, 0:half, :] = zero_half
                padded[snap, field, y, half + cells_x : 2 * half + cells_x, :] = zero_half
    for level in range(steps):
        for field in (SRC, RCV):
            for y in range(REACH, REACH + slab_y):
                levels[level, field, y, 0:EDGE, :] = zero_edge
                levels[level, field, y, EDGE + cells_x : EDGE + cells_x + EDGE, :] = zero_edge

    @pl.when(me == 0)
    def _():
        for level in range(steps):
            for field in (SRC, RCV):
                for y in range(REACH):
                    levels[level, field, y, inside, :] = zero_plane

    @pl.when(me == devices - 1)
    def _():
        for level in range(steps):
            for field in (SRC, RCV):
                for y in range(REACH):
                    levels[level, field, REACH + slab_y + y, inside, :] = zero_plane

    loads[0].wait()
    loads[1].wait()

    for peer in range(devices):
        first = peer * slab_y - REACH
        low, high = max(first, 0), min(first + span, cells_y)
        for x in range(slab_x):
            base = (peer * slab_x + x) * rows
            if low > first or high < first + span:
                staged[base : base + rows, :] = jnp.zeros((rows, cells_z), jnp.float32)
            staged[base + low - first : base + high - first, :] = src_now[x, low:high, :]
            staged[base + span : base + span + slab_y, :] = src_old[
                x, peer * slab_y : (peer + 1) * slab_y, :
            ]

    for load in loads[3:]:
        load.wait()
    row_at = lax.broadcasted_iota(jnp.int32, (cells_x, cells_z), 0)
    lane_at = lax.broadcasted_iota(jnp.int32, (cells_x, cells_z), 1)
    column = ((row_at == shot[0]) & (lane_at == shot[2])).astype(jnp.float32)
    for y in range(slab_y):
        spot[y] = column * (me * slab_y + y == shot[1]).astype(jnp.float32)
    x_at = lax.broadcasted_iota(jnp.int32, (cells_x, traces.shape[2]), 0)
    for y in range(slab_y):
        onehot = (x_at == rec_x[y : y + 1, :]).astype(jnp.float32)
        for step in range(steps):
            total = jnp.sum(onehot * traces[y, step : step + 1, :], axis=1, keepdims=True)
            surface[step, y] = jnp.where(lane_at == 0, total, 0.0)
    loads[2].wait()

    pl.semaphore_wait(barrier, devices - 1)

    def out_copy(peer):
        return pltpu.make_async_remote_copy(
            src_ref=staged.at[pl.ds(pl.multiple_of(peer * block, 8), block)],
            dst_ref=landed.at[pl.ds(pl.multiple_of(me * block, 8), block)],
            send_sem=out_send,
            recv_sem=out_recv,
            device_id={"wide": peer},
            device_id_type=MESH,
        )

    def halo_copy(field, level, side):
        first = slab_y if side == 0 else REACH
        source = levels.at[level, field, pl.ds(first, REACH), inside]
        into = 0 if side == 0 else REACH + slab_y
        peer = me + 1 if side == 0 else me - 1
        return pltpu.make_async_remote_copy(
            src_ref=source,
            dst_ref=levels.at[level, field, pl.ds(into, REACH), inside],
            send_sem=halo_send.at[field, level, side],
            recv_sem=halo_recv.at[field, level, side],
            device_id={"wide": peer},
            device_id_type=MESH,
        )

    def each_side(field, level, act):
        @pl.when(me < devices - 1)
        def _():
            act(0)

        @pl.when(me > 0)
        def _():
            act(1)

    def send_halo(field, level):
        each_side(field, level, lambda side: halo_copy(field, level, side).start())

    def wait_halo(field, level):
        each_side(field, level, lambda side: halo_copy(field, level, 1 - side).wait_recv())

    def wait_sent(field, level):
        each_side(field, level, lambda side: halo_copy(field, level, side).wait_send())

    for distance in far_first:
        out_copy(lax.rem(me + distance, devices)).start()

    send_halo(RCV, 0)

    own = pl.ds(pl.multiple_of(me * block, 8), block)
    landed[own, :] = staged[own, :]

    def older(field, level, y):
        if level > 0:
            return levels[level - 1, field, REACH + y, inside, :]
        if field == RCV:
            return rcv_old[y]
        return landed[pl.ds(span + y, cells_x, stride=rows), :]

    def local(field, level):
        for y in range(slab_y):
            centre = levels[level, field, REACH + y, inside, :]

            def along_x(shift):
                if shift == 0:
                    return centre
                return levels[level, field, REACH + y, pl.ds(EDGE + shift, cells_x), :]

            def along_z(shift):
                if shift == 0:
                    return centre
                turned = pltpu.roll(centre, (-shift) % cells_z, 1)
                kept = lane_at >= -shift if shift < 0 else lane_at < cells_z - shift
                return jnp.where(kept, turned, 0.0)

            partial[field, y] = (
                2.0 * centre
                - older(field, level, y)
                + medium[0, y] * second(along_x)
                + medium[2, y] * second(along_z)
            )

    def finish(field, level):
        for y in range(slab_y):
            def along_y(shift):
                return levels[level, field, REACH + y + shift, inside, :]

            if field == SRC:
                added = -wavelet[level] * spot[y]
            else:
                added = surface[level, y]
            levels[level + 1, field, REACH + y, inside, :] = (
                partial[field, y] + medium[1, y] * second(along_y) + added
            )

    local(RCV, 0)
    wait_halo(RCV, 0)
    finish(RCV, 0)
    send_halo(RCV, 1)
    local(RCV, 1)

    arrived = landed.at[pl.ds(0, (devices - 1) * block)]
    pltpu.make_async_copy(arrived, arrived, out_recv).wait()
    for y in range(span):
        levels[0, SRC, y, inside, :] = landed[pl.ds(y, cells_x, stride=rows), :]
    local(SRC, 0)
    finish(SRC, 0)
    for level in range(1, steps):
        send_halo(SRC, level)
        local(SRC, level)
        wait_halo(RCV, level)
        finish(RCV, level)
        if level + 1 < steps:
            send_halo(RCV, level + 1)
            local(RCV, level + 1)
        wait_halo(SRC, level)
        finish(SRC, level)

    for back, level in enumerate((steps, steps - 1)):
        for x in range(slab_x):
            for y in range(slab_y):
                at = (back * slab_x + x) * slab_y + y
                leaving[pl.ds(at, devices, stride=back_rows), :] = levels[
                    level, SRC, REACH + y, pl.ds(EDGE + x, devices, stride=slab_x), :
                ]

    def back_copy(peer):
        return pltpu.make_async_remote_copy(
            src_ref=leaving.at[pl.ds(pl.multiple_of(peer * back_rows, 8), back_rows)],
            dst_ref=returned.at[pl.ds(pl.multiple_of(me * back_rows, 8), back_rows)],
            send_sem=back_send,
            recv_sem=back_recv,
            device_id={"wide": peer},
            device_id_type=MESH,
        )

    for distance in far_first:
        back_copy(lax.rem(me + distance, devices)).start()

    own_back = pl.ds(pl.multiple_of(me * back_rows, 8), back_rows)
    returned[own_back, :] = leaving[own_back, :]
    for y in range(slab_y):
        rcv_next[y] = levels[steps, RCV, REACH + y, inside, :]
        rcv_prior[y] = levels[steps - 1, RCV, REACH + y, inside, :]
        for field in (SRC, RCV):
            for snap in range(padded.shape[0]):
                padded[snap, field, y, half : half + cells_x, :] = levels[
                    2 * snap + 2, field, REACH + y, inside, :
                ]
    for plane in range(lags):
        slot = lag_order[plane]
        at_src = pl.ds(2 * half - slot, cells_x)
        at_rcv = pl.ds(slot, cells_x)
        for y in range(slab_y):
            total = None
            for snap in range(padded.shape[0]):
                product = padded[snap, SRC, y, at_src, :] * padded[snap, RCV, y, at_rcv, :]
                total = product if total is None else total + product
            board[plane, y] = total

    sent = staged.at[pl.ds(0, (devices - 1) * block)]
    pltpu.make_async_copy(sent, sent, out_send).wait()
    for level in range(steps):
        wait_sent(RCV, level)
        if level > 0:
            wait_sent(SRC, level)

    came = returned.at[pl.ds(0, (devices - 1) * back_rows)]
    pltpu.make_async_copy(came, came, back_recv).wait()
    for back, result in enumerate((src_next, src_prior)):
        for x in range(slab_x):
            for y in range(slab_y):
                at = (back * slab_x + x) * slab_y + y
                result[x, pl.ds(y, devices, stride=slab_y), :] = returned[
                    pl.ds(at, devices, stride=back_rows), :
                ]
    gone = leaving.at[pl.ds(0, (devices - 1) * back_rows)]
    pltpu.make_async_copy(gone, gone, back_send).wait()


def deliver_kernel(*refs):
    count = (len(refs) - 1) // 2
    copies = [
        pltpu.make_async_copy(refs[i], refs[count + i], refs[-1].at[i]) for i in range(count)
    ]
    for copy in copies:
        copy.start()
    for copy in copies:
        copy.wait()


MESH = pl.DeviceIdType.MESH


def solution(mesh):
    devices = mesh.shape["wide"]

    def on_device(
        src_now, src_old, rcv_now, rcv_old, medium, wavelet, shot, traces, rec_x, lag_order
    ):
        slab_x, cells_y, cells_z = src_now.shape
        slab_y, _, cells_x = rcv_now.shape
        steps = wavelet.shape[0]
        lags = lag_order.shape[0]
        half = (lags - 1) // 2
        span = slab_y + 2 * REACH
        rows = -(-(span + slab_y) // 8) * 8
        f32 = jnp.float32
        vmem = pl.BlockSpec(memory_space=pltpu.VMEM)
        hbm = pl.BlockSpec(memory_space=pltpu.HBM)
        src_shape = jax.ShapeDtypeStruct((slab_x, cells_y, cells_z), f32)
        rcv_shape = jax.ShapeDtypeStruct((slab_y, cells_x, cells_z), f32)
        board_shape = jax.ShapeDtypeStruct((lags, slab_y, cells_x, cells_z), f32)
        shapes = (src_shape, src_shape, rcv_shape, rcv_shape, board_shape)
        taken = steps // 2
        turn = lambda array: jnp.swapaxes(array, -1, -2)
        like = lambda array: pltpu.VMEM(array.shape, array.dtype)
        scalars = lambda array: pltpu.SMEM(array.shape, array.dtype)
        rcv_now, rcv_old, medium, traces = map(turn, (rcv_now, rcv_old, medium, traces))
        scratch = [
            like(src_now),
            like(src_old),
            like(rcv_old),
            like(medium),
            scalars(wavelet),
            scalars(shot),
            like(traces),
            like(rec_x),
            scalars(lag_order),
            pltpu.VMEM((taken, 2, slab_y, cells_x + 2 * half, cells_z), f32),
            pltpu.VMEM((cells_x * rows, cells_z), f32),
            pltpu.VMEM((cells_x * rows, cells_z), f32),
            pltpu.VMEM((steps + 1, 2, span, cells_x + 2 * EDGE, cells_z), f32),
            pltpu.VMEM((2, slab_y, cells_x, cells_z), f32),
            pltpu.VMEM((steps, slab_y, cells_x, cells_z), f32),
            pltpu.VMEM((slab_y, cells_x, cells_z), f32),
            pltpu.VMEM((devices * 2 * slab_x * slab_y, cells_z), f32),
            pltpu.VMEM((devices * 2 * slab_x * slab_y, cells_z), f32),
        ]
        held = sum(4 * math.prod(each.shape) for each in scratch + list(shapes))
        results = pl.pallas_call(
            functools.partial(window_kernel, devices),
            out_shape=shapes,
            in_specs=[hbm] * 10,
            out_specs=(vmem,) * 5,
            scratch_shapes=scratch
            + [pltpu.SemaphoreType.DMA] * 4
            + [
                pltpu.SemaphoreType.DMA((2, steps, 2)),
                pltpu.SemaphoreType.DMA((2, steps, 2)),
                pltpu.SemaphoreType.DMA((10,)),
            ],
            compiler_params=pltpu.CompilerParams(
                collective_id=0, has_side_effects=True, vmem_limit_bytes=held + (4 << 20)
            ),
            name="window",
        )(
            *(
                pltpu.with_memory_space_constraint(array, pltpu.HBM)
                for array in (
                    src_now,
                    src_old,
                    rcv_now,
                    rcv_old,
                    medium,
                    wavelet,
                    shot,
                    traces,
                    rec_x,
                    lag_order,
                )
            )
        )
        outs = pl.pallas_call(
            deliver_kernel,
            out_shape=shapes,
            in_specs=[vmem] * 5,
            out_specs=(hbm,) * 5,
            scratch_shapes=[pltpu.SemaphoreType.DMA((5,))],
            compiler_params=pltpu.CompilerParams(vmem_limit_bytes=held + (4 << 20)),
            name="deliver",
        )(*results)
        return outs[0], outs[1], turn(outs[2]), turn(outs[3]), turn(outs[4])

    return jax.shard_map(
        on_device,
        mesh=mesh,
        in_specs=(
            P("wide", "shots", None),
            P("wide", "shots", None),
            P("wide", "shots", None),
            P("wide", "shots", None),
            P(None, "wide", None, None),
            P(),
            P("shots"),
            P("wide", "shots", None),
            P("wide", "shots"),
            P(),
        ),
        out_specs=(
            P("wide", "shots", None),
            P("wide", "shots", None),
            P("wide", "shots", None),
            P("wide", "shots", None),
            P("shots", "wide", None, None),
        ),
        check_vma=False,
    )
```

```python
import functools
import math

import jax
import jax.numpy as jnp
from jax import lax
from jax.experimental import pallas as pl
from jax.experimental.pallas import tpu as pltpu
from jax.sharding import PartitionSpec as P

REACH = 2
EDGE = 8
OUTER, INNER, CENTRE = -1.0 / 12.0, 4.0 / 3.0, -2.5
SRC, RCV = 0, 1


def second(window):
    return (
        OUTER * (window(-2) + window(2)) + INNER * (window(-1) + window(1)) + CENTRE * window(0)
    )


def window_kernel(
    devices,
    src_now_in,
    src_old_in,
    rcv_now_in,
    rcv_old_in,
    medium_in,
    wavelet_in,
    shot_in,
    traces_in,
    rec_x_in,
    lag_order_in,
    src_next,
    src_prior,
    rcv_next,
    rcv_prior,
    board,
    src_now,
    src_old,
    rcv_old,
    medium,
    wavelet,
    shot,
    traces,
    rec_x,
    lag_order,
    padded,
    staged,
    landed,
    levels,
    partial,
    surface,
    spot,
    leaving,
    returned,
    out_send,
    out_recv,
    back_send,
    back_recv,
    halo_send,
    halo_recv,
    load_sems,
    side_send,
    side_recv,
):
    me = lax.axis_index("wide")
    slab_x, cells_y, cells_z = src_now.shape
    slab_y, cells_x, _ = rcv_old.shape
    steps = wavelet.shape[0]
    span = slab_y + 2 * REACH
    pad = 2 * REACH
    rows = staged.shape[0] // (devices * slab_x)
    block = slab_x * rows
    back_rows = 2 * slab_x * slab_y
    inside = pl.ds(EDGE, cells_x)

    lags = lag_order.shape[0]
    half = (lags - 1) // 2
    middle = devices // 2
    far_first = sorted(range(1, devices), key=lambda distance: abs(distance - middle))

    loads = []
    for index, (source, target) in enumerate(
        (
            (src_now_in, src_now),
            (src_old_in, src_old),
            (rcv_now_in, levels.at[0, RCV, pl.ds(pad, slab_y), inside]),
            (shot_in, shot),
            (traces_in, traces),
            (rec_x_in, rec_x),
            (rcv_old_in, rcv_old),
            (medium_in, medium.at[:, pl.ds(REACH, slab_y)]),
            (wavelet_in, wavelet),
            (lag_order_in, lag_order),
        )
    ):
        loads.append(pltpu.make_async_copy(source, target, load_sems.at[index]))
    for load in loads[:3]:
        load.start()

    barrier = pltpu.get_barrier_semaphore()
    for distance in far_first:
        pl.semaphore_signal(
            barrier,
            inc=1,
            device_id={"wide": lax.rem(me + distance, devices)},
            device_id_type=MESH,
        )
    for load in loads[3:]:
        load.start()

    zero_edge = jnp.zeros((EDGE, cells_z), jnp.float32)
    zero_plane = jnp.zeros((cells_x, cells_z), jnp.float32)
    zero_half = jnp.zeros((half, cells_z), jnp.float32)
    for snap in range(padded.shape[0]):
        for field in (SRC, RCV):
            for y in range(slab_y):
                padded[snap, field, y, 0:half, :] = zero_half
                padded[snap, field, y, half + cells_x : 2 * half + cells_x, :] = zero_half
    for level in range(steps):
        for field in (SRC, RCV):
            for y in range(REACH, REACH + span):
                levels[level, field, y, 0:EDGE, :] = zero_edge
                levels[level, field, y, EDGE + cells_x : EDGE + cells_x + EDGE, :] = zero_edge

    def clear(near, planes):
        @pl.when(near)
        def _():
            for level in range(steps):
                for field in (SRC, RCV):
                    for plane in planes:
                        levels[level, field, plane, inside, :] = zero_plane

    clear(me < 2, range(REACH))
    clear(me < 1, range(REACH, pad))
    clear(me >= devices - 2, range(pad + 2 * slab_y, 2 * pad + slab_y))
    clear(me >= devices - 1, range(pad + slab_y, pad + 2 * slab_y))

    loads[0].wait()
    loads[1].wait()

    for peer in range(devices):
        first = peer * slab_y - REACH
        low, high = max(first, 0), min(first + span, cells_y)
        for x in range(slab_x):
            base = (peer * slab_x + x) * rows
            if low > first or high < first + span:
                staged[base : base + rows, :] = jnp.zeros((rows, cells_z), jnp.float32)
            staged[base + low - first : base + high - first, :] = src_now[x, low:high, :]
            staged[base + span : base + span + slab_y, :] = src_old[
                x, peer * slab_y : (peer + 1) * slab_y, :
            ]

    for load in loads[3:]:
        load.wait()
    row_at = lax.broadcasted_iota(jnp.int32, (cells_x, cells_z), 0)
    lane_at = lax.broadcasted_iota(jnp.int32, (cells_x, cells_z), 1)
    column = ((row_at == shot[0]) & (lane_at == shot[2])).astype(jnp.float32)
    for y in range(-REACH, slab_y + REACH):
        spot[REACH + y] = column * (me * slab_y + y == shot[1]).astype(jnp.float32)
    x_at = lax.broadcasted_iota(jnp.int32, (cells_x, traces.shape[2]), 0)
    for y in range(slab_y):
        onehot = (x_at == rec_x[y : y + 1, :]).astype(jnp.float32)
        for step in range(steps):
            total = jnp.sum(onehot * traces[y, step : step + 1, :], axis=1, keepdims=True)
            surface[step, REACH + y] = jnp.where(lane_at == 0, total, 0.0)
    loads[2].wait()

    pl.semaphore_wait(barrier, devices - 1)

    def out_copy(peer):
        return pltpu.make_async_remote_copy(
            src_ref=staged.at[pl.ds(pl.multiple_of(peer * block, 8), block)],
            dst_ref=landed.at[pl.ds(pl.multiple_of(me * block, 8), block)],
            send_sem=out_send,
            recv_sem=out_recv,
            device_id={"wide": peer},
            device_id_type=MESH,
        )

    def send_to(hop, side, source, target, send_sem, recv_sem):
        return pltpu.make_async_remote_copy(
            src_ref=source,
            dst_ref=target,
            send_sem=send_sem,
            recv_sem=recv_sem,
            device_id={"wide": me + hop if side == 0 else me - hop},
            device_id_type=MESH,
        )

    def halo_copy(field, level, hop, side):
        into = pad - hop * slab_y if side == 0 else pad + hop * slab_y
        return send_to(
            hop,
            side,
            levels.at[level, field, pl.ds(pad, slab_y), inside],
            levels.at[level, field, pl.ds(into, slab_y), inside],
            halo_send.at[field, level, hop - 1, side],
            halo_recv.at[field, level, hop - 1, side],
        )

    def side_copy(kind, side):
        into = pl.ds(0 if side == 0 else REACH + slab_y, slab_y)
        whole = medium if kind == 0 else surface
        lead = pl.ds(0, 3) if kind == 0 else pl.ds(1, steps - 3)
        return send_to(
            1,
            side,
            whole.at[lead, pl.ds(REACH, slab_y)],
            whole.at[lead, into],
            side_send.at[kind, side],
            side_recv.at[kind, side],
        )

    def each_side(hop, act):
        @pl.when(me < devices - hop)
        def _():
            act(0)

        @pl.when(me >= hop)
        def _():
            act(1)

    def wide(level):
        return level % 2 == 1 and level + 1 < steps

    def hops(level):
        return (1, 2) if wide(level) else (1,) if level % 2 == 1 else ()

    def send_halo(field, level, reach):
        for hop in reach:
            each_side(hop, lambda side: halo_copy(field, level, hop, side).start())

    def wait_halo(field, level, reach):
        for hop in reach:
            each_side(hop, lambda side: halo_copy(field, level, hop, 1 - side).wait_recv())

    def wait_sent(field, level, reach):
        for hop in reach:
            each_side(hop, lambda side: halo_copy(field, level, hop, side).wait_send())

    for distance in far_first:
        out_copy(lax.rem(me + distance, devices)).start()

    send_halo(RCV, 0, (1,))
    for kind in range(2):
        each_side(1, lambda side: side_copy(kind, side).start())

    own = pl.ds(pl.multiple_of(me * block, 8), block)
    landed[own, :] = staged[own, :]

    def older(field, level, y):
        if level > 0:
            return levels[level - 1, field, pad + y, inside, :]
        if field == RCV:
            return rcv_old[y]
        return landed[pl.ds(span + y, cells_x, stride=rows), :]

    def local(field, level, planes):
        for y in planes:
            centre = levels[level, field, pad + y, inside, :]

            def along_x(shift):
                if shift == 0:
                    return centre
                return levels[level, field, pad + y, pl.ds(EDGE + shift, cells_x), :]

            def along_z(shift):
                if shift == 0:
                    return centre
                turned = pltpu.roll(centre, (-shift) % cells_z, 1)
                kept = lane_at >= -shift if shift < 0 else lane_at < cells_z - shift
                return jnp.where(kept, turned, 0.0)

            partial[field, REACH + y] = (
                2.0 * centre
                - older(field, level, y)
                + medium[0, REACH + y] * second(along_x)
                + medium[2, REACH + y] * second(along_z)
            )

    def finish(field, level, planes):
        for y in planes:
            def along_y(shift):
                return levels[level, field, pad + y + shift, inside, :]

            if field == SRC:
                added = -wavelet[level] * spot[REACH + y]
            else:
                added = surface[level, REACH + y]
            levels[level + 1, field, pad + y, inside, :] = (
                partial[field, REACH + y] + medium[1, REACH + y] * second(along_y) + added
            )

    mine = range(slab_y)

    def around(field, level):
        def act(side):
            planes = range(slab_y, slab_y + REACH) if side == 0 else range(-REACH, 0)
            local(field, level, planes)
            finish(field, level, planes)

        each_side(1, act)

    local(RCV, 0, mine)
    wait_halo(RCV, 0, (1,))
    finish(RCV, 0, mine)
    send_halo(RCV, 1, hops(1))
    local(RCV, 1, mine)

    arrived = landed.at[pl.ds(0, (devices - 1) * block)]
    pltpu.make_async_copy(arrived, arrived, out_recv).wait()
    for y in range(span):
        levels[0, SRC, REACH + y, inside, :] = landed[pl.ds(y, cells_x, stride=rows), :]
    local(SRC, 0, mine)
    finish(SRC, 0, mine)
    for level in range(1, steps):
        send_halo(SRC, level, hops(level))
        local(SRC, level, mine)
        wait_halo(RCV, level, hops(level))
        finish(RCV, level, mine)
        if level + 1 < steps:
            send_halo(RCV, level + 1, hops(level + 1))
            local(RCV, level + 1, mine)
        if level == 1:
            for kind in range(2):
                each_side(1, lambda side: side_copy(kind, 1 - side).wait_recv())
        if wide(level):
            around(RCV, level)
        wait_halo(SRC, level, hops(level))
        finish(SRC, level, mine)
        if wide(level):
            around(SRC, level)

    for back, level in enumerate((steps, steps - 1)):
        for x in range(slab_x):
            for y in range(slab_y):
                at = (back * slab_x + x) * slab_y + y
                leaving[pl.ds(at, devices, stride=back_rows), :] = levels[
                    level, SRC, pad + y, pl.ds(EDGE + x, devices, stride=slab_x), :
                ]

    def back_copy(peer):
        return pltpu.make_async_remote_copy(
            src_ref=leaving.at[pl.ds(pl.multiple_of(peer * back_rows, 8), back_rows)],
            dst_ref=returned.at[pl.ds(pl.multiple_of(me * back_rows, 8), back_rows)],
            send_sem=back_send,
            recv_sem=back_recv,
            device_id={"wide": peer},
            device_id_type=MESH,
        )

    for distance in far_first:
        back_copy(lax.rem(me + distance, devices)).start()

    own_back = pl.ds(pl.multiple_of(me * back_rows, 8), back_rows)
    returned[own_back, :] = leaving[own_back, :]
    for y in range(slab_y):
        rcv_next[y] = levels[steps, RCV, pad + y, inside, :]
        rcv_prior[y] = levels[steps - 1, RCV, pad + y, inside, :]
        for field in (SRC, RCV):
            for snap in range(padded.shape[0]):
                padded[snap, field, y, half : half + cells_x, :] = levels[
                    2 * snap + 2, field, pad + y, inside, :
                ]
    for plane in range(lags):
        slot = lag_order[plane]
        at_src = pl.ds(2 * half - slot, cells_x)
        at_rcv = pl.ds(slot, cells_x)
        for y in range(slab_y):
            total = None
            for snap in range(padded.shape[0]):
                product = padded[snap, SRC, y, at_src, :] * padded[snap, RCV, y, at_rcv, :]
                total = product if total is None else total + product
            board[plane, y] = total

    sent = staged.at[pl.ds(0, (devices - 1) * block)]
    pltpu.make_async_copy(sent, sent, out_send).wait()
    for level in range(steps):
        wait_sent(RCV, level, hops(level) if level > 0 else (1,))
        wait_sent(SRC, level, hops(level))
    for kind in range(2):
        each_side(1, lambda side: side_copy(kind, side).wait_send())

    came = returned.at[pl.ds(0, (devices - 1) * back_rows)]
    pltpu.make_async_copy(came, came, back_recv).wait()
    for back, result in enumerate((src_next, src_prior)):
        for x in range(slab_x):
            for y in range(slab_y):
                at = (back * slab_x + x) * slab_y + y
                result[x, pl.ds(y, devices, stride=slab_y), :] = returned[
                    pl.ds(at, devices, stride=back_rows), :
                ]
    gone = leaving.at[pl.ds(0, (devices - 1) * back_rows)]
    pltpu.make_async_copy(gone, gone, back_send).wait()


def deliver_kernel(*refs):
    count = (len(refs) - 1) // 2
    copies = [
        pltpu.make_async_copy(refs[i], refs[count + i], refs[-1].at[i]) for i in range(count)
    ]
    for copy in copies:
        copy.start()
    for copy in copies:
        copy.wait()


MESH = pl.DeviceIdType.MESH


def solution(mesh):
    devices = mesh.shape["wide"]

    def on_device(
        src_now, src_old, rcv_now, rcv_old, medium, wavelet, shot, traces, rec_x, lag_order
    ):
        slab_x, cells_y, cells_z = src_now.shape
        slab_y, _, cells_x = rcv_now.shape
        steps = wavelet.shape[0]
        lags = lag_order.shape[0]
        half = (lags - 1) // 2
        assert slab_y == REACH and devices > 3
        span = slab_y + 2 * REACH
        rows = -(-(span + slab_y) // 8) * 8
        f32 = jnp.float32
        vmem = pl.BlockSpec(memory_space=pltpu.VMEM)
        hbm = pl.BlockSpec(memory_space=pltpu.HBM)
        src_shape = jax.ShapeDtypeStruct((slab_x, cells_y, cells_z), f32)
        rcv_shape = jax.ShapeDtypeStruct((slab_y, cells_x, cells_z), f32)
        board_shape = jax.ShapeDtypeStruct((lags, slab_y, cells_x, cells_z), f32)
        shapes = (src_shape, src_shape, rcv_shape, rcv_shape, board_shape)
        taken = steps // 2
        turn = lambda array: jnp.swapaxes(array, -1, -2)
        like = lambda array: pltpu.VMEM(array.shape, array.dtype)
        scalars = lambda array: pltpu.SMEM(array.shape, array.dtype)
        rcv_now, rcv_old, medium, traces = map(turn, (rcv_now, rcv_old, medium, traces))
        scratch = [
            like(src_now),
            like(src_old),
            like(rcv_old),
            pltpu.VMEM((3, span, cells_x, cells_z), f32),
            scalars(wavelet),
            scalars(shot),
            like(traces),
            like(rec_x),
            scalars(lag_order),
            pltpu.VMEM((taken, 2, slab_y, cells_x + 2 * half, cells_z), f32),
            pltpu.VMEM((cells_x * rows, cells_z), f32),
            pltpu.VMEM((cells_x * rows, cells_z), f32),
            pltpu.VMEM((steps + 1, 2, span + 2 * REACH, cells_x + 2 * EDGE, cells_z), f32),
            pltpu.VMEM((2, span, cells_x, cells_z), f32),
            pltpu.VMEM((steps, span, cells_x, cells_z), f32),
            pltpu.VMEM((span, cells_x, cells_z), f32),
            pltpu.VMEM((devices * 2 * slab_x * slab_y, cells_z), f32),
            pltpu.VMEM((devices * 2 * slab_x * slab_y, cells_z), f32),
        ]
        held = sum(4 * math.prod(each.shape) for each in scratch + list(shapes))
        results = pl.pallas_call(
            functools.partial(window_kernel, devices),
            out_shape=shapes,
            in_specs=[hbm] * 10,
            out_specs=(vmem,) * 5,
            scratch_shapes=scratch
            + [pltpu.SemaphoreType.DMA] * 4
            + [
                pltpu.SemaphoreType.DMA((2, steps, 2, 2)),
                pltpu.SemaphoreType.DMA((2, steps, 2, 2)),
                pltpu.SemaphoreType.DMA((10,)),
                pltpu.SemaphoreType.DMA((2, 2)),
                pltpu.SemaphoreType.DMA((2, 2)),
            ],
            compiler_params=pltpu.CompilerParams(
                collective_id=0, has_side_effects=True, vmem_limit_bytes=held + (4 << 20)
            ),
            name="window",
        )(
            *(
                pltpu.with_memory_space_constraint(array, pltpu.HBM)
                for array in (
                    src_now,
                    src_old,
                    rcv_now,
                    rcv_old,
                    medium,
                    wavelet,
                    shot,
                    traces,
                    rec_x,
                    lag_order,
                )
            )
        )
        outs = pl.pallas_call(
            deliver_kernel,
            out_shape=shapes,
            in_specs=[vmem] * 5,
            out_specs=(hbm,) * 5,
            scratch_shapes=[pltpu.SemaphoreType.DMA((5,))],
            compiler_params=pltpu.CompilerParams(vmem_limit_bytes=held + (4 << 20)),
            name="deliver",
        )(*results)
        return outs[0], outs[1], turn(outs[2]), turn(outs[3]), turn(outs[4])

    return jax.shard_map(
        on_device,
        mesh=mesh,
        in_specs=(
            P("wide", "shots", None),
            P("wide", "shots", None),
            P("wide", "shots", None),
            P("wide", "shots", None),
            P(None, "wide", None, None),
            P(),
            P("shots"),
            P("wide", "shots", None),
            P("wide", "shots"),
            P(),
        ),
        out_specs=(
            P("wide", "shots", None),
            P("wide", "shots", None),
            P("wide", "shots", None),
            P("wide", "shots", None),
            P("shots", "wide", None, None),
        ),
        check_vma=False,
    )
```

```python
import functools
import math

import jax
import jax.numpy as jnp
from jax import lax
from jax.experimental import pallas as pl
from jax.experimental.pallas import tpu as pltpu
from jax.sharding import PartitionSpec as P

REACH = 2
EDGE = 8
OUTER, INNER, CENTRE = -1.0 / 12.0, 4.0 / 3.0, -2.5
SRC, RCV = 0, 1
PARTS = 6


def second(window):
    return (
        OUTER * (window(-2) + window(2)) + INNER * (window(-1) + window(1)) + CENTRE * window(0)
    )


def window_kernel(
    devices,
    src_now_in,
    src_old_in,
    rcv_now_in,
    rcv_old_in,
    medium_in,
    wavelet_in,
    shot_in,
    traces_in,
    rec_x_in,
    lag_order_in,
    src_next,
    src_prior,
    rcv_next,
    rcv_prior,
    board,
    src_now,
    src_old,
    rcv_old,
    medium,
    wavelet,
    shot,
    traces,
    rec_x,
    lag_order,
    padded,
    staged,
    landed,
    levels,
    partial,
    surface,
    spot,
    leaving,
    returned,
    out_send,
    out_recv,
    back_send,
    back_recv,
    halo_send,
    halo_recv,
    load_sems,
):
    me = lax.axis_index("wide")
    slab_x, cells_y, cells_z = src_now.shape
    slab_y, cells_x, _ = rcv_old.shape
    steps = wavelet.shape[0]
    span = slab_y + 2 * REACH
    rows = staged.shape[0] // (devices * slab_x)
    block = slab_x * rows
    back_rows = 2 * slab_x * slab_y
    inside = pl.ds(EDGE, cells_x)

    lags = lag_order.shape[0]
    half = (lags - 1) // 2
    middle = devices // 2
    far_first = sorted(range(1, devices), key=lambda distance: abs(distance - middle))

    loads = []
    for index, (source, target) in enumerate(
        (
            (src_now_in, src_now),
            (src_old_in, src_old),
            (rcv_now_in, levels.at[0, RCV, pl.ds(REACH, slab_y), inside]),
            (shot_in, shot),
            (traces_in, traces),
            (rec_x_in, rec_x),
            (rcv_old_in, rcv_old),
            (medium_in, medium),
            (wavelet_in, wavelet),
            (lag_order_in, lag_order),
        )
    ):
        loads.append(pltpu.make_async_copy(source, target, load_sems.at[index]))
    for load in loads[:3]:
        load.start()

    barrier = pltpu.get_barrier_semaphore()
    for distance in far_first:
        pl.semaphore_signal(
            barrier,
            inc=1,
            device_id={"wide": lax.rem(me + distance, devices)},
            device_id_type=MESH,
        )
    for load in loads[3:]:
        load.start()

    zero_edge = jnp.zeros((EDGE, cells_z), jnp.float32)
    zero_plane = jnp.zeros((cells_x, cells_z), jnp.float32)
    zero_half = jnp.zeros((half, cells_z), jnp.float32)
    for snap in range(padded.shape[0]):
        for field in (SRC, RCV):
            for y in range(slab_y):
                padded[snap, field, y, 0:half, :] = zero_half
                padded[snap, field, y, half + cells_x : 2 * half + cells_x, :] = zero_half
    for level in range(steps):
        for field in (SRC, RCV):
            for y in range(REACH, REACH + slab_y):
                levels[level, field, y, 0:EDGE, :] = zero_edge
                levels[level, field, y, EDGE + cells_x : EDGE + cells_x + EDGE, :] = zero_edge

    @pl.when(me == 0)
    def _():
        for level in range(steps):
            for field in (SRC, RCV):
                for y in range(REACH):
                    levels[level, field, y, inside, :] = zero_plane

    @pl.when(me == devices - 1)
    def _():
        for level in range(steps):
            for field in (SRC, RCV):
                for y in range(REACH):
                    levels[level, field, REACH + slab_y + y, inside, :] = zero_plane

    loads[0].wait()
    loads[1].wait()

    for peer in range(devices):
        first = peer * slab_y - REACH
        low, high = max(first, 0), min(first + span, cells_y)
        for x in range(slab_x):
            base = (peer * slab_x + x) * rows
            if low > first or high < first + span:
                staged[base : base + rows, :] = jnp.zeros((rows, cells_z), jnp.float32)
            staged[base + low - first : base + high - first, :] = src_now[x, low:high, :]
            staged[base + span : base + span + slab_y, :] = src_old[
                x, peer * slab_y : (peer + 1) * slab_y, :
            ]

    for load in loads[3:]:
        load.wait()
    row_at = lax.broadcasted_iota(jnp.int32, (cells_x, cells_z), 0)
    lane_at = lax.broadcasted_iota(jnp.int32, (cells_x, cells_z), 1)
    column = ((row_at == shot[0]) & (lane_at == shot[2])).astype(jnp.float32)
    for y in range(slab_y):
        spot[y] = column * (me * slab_y + y == shot[1]).astype(jnp.float32)
    x_at = lax.broadcasted_iota(jnp.int32, (cells_x, traces.shape[2]), 0)
    for y in range(slab_y):
        onehot = (x_at == rec_x[y : y + 1, :]).astype(jnp.float32)
        for step in range(steps):
            total = jnp.sum(onehot * traces[y, step : step + 1, :], axis=1, keepdims=True)
            surface[step, y] = jnp.where(lane_at == 0, total, 0.0)
    loads[2].wait()

    pl.semaphore_wait(barrier, devices - 1)

    def out_copy(peer):
        return pltpu.make_async_remote_copy(
            src_ref=staged.at[pl.ds(pl.multiple_of(peer * block, 8), block)],
            dst_ref=landed.at[pl.ds(pl.multiple_of(me * block, 8), block)],
            send_sem=out_send,
            recv_sem=out_recv,
            device_id={"wide": peer},
            device_id_type=MESH,
        )

    def halo_copy(field, level, side):
        first = slab_y if side == 0 else REACH
        source = levels.at[level, field, pl.ds(first, REACH), inside]
        into = 0 if side == 0 else REACH + slab_y
        peer = me + 1 if side == 0 else me - 1
        return pltpu.make_async_remote_copy(
            src_ref=source,
            dst_ref=levels.at[level, field, pl.ds(into, REACH), inside],
            send_sem=halo_send.at[field, level, side],
            recv_sem=halo_recv.at[field, level, side],
            device_id={"wide": peer},
            device_id_type=MESH,
        )

    def each_side(field, level, act):
        @pl.when(me < devices - 1)
        def _():
            act(0)

        @pl.when(me > 0)
        def _():
            act(1)

    def send_halo(field, level):
        each_side(field, level, lambda side: halo_copy(field, level, side).start())

    def wait_halo(field, level):
        each_side(field, level, lambda side: halo_copy(field, level, 1 - side).wait_recv())

    def wait_sent(field, level):
        each_side(field, level, lambda side: halo_copy(field, level, side).wait_send())

    for distance in far_first:
        out_copy(lax.rem(me + distance, devices)).start()

    send_halo(RCV, 0)

    own = pl.ds(pl.multiple_of(me * block, 8), block)
    landed[own, :] = staged[own, :]

    def older(field, level, y):
        if level > 0:
            return levels[level - 1, field, REACH + y, inside, :]
        if field == RCV:
            return rcv_old[y]
        return landed[pl.ds(span + y, cells_x, stride=rows), :]

    def local(field, level):
        for y in range(slab_y):
            centre = levels[level, field, REACH + y, inside, :]

            def along_x(shift):
                if shift == 0:
                    return centre
                return levels[level, field, REACH + y, pl.ds(EDGE + shift, cells_x), :]

            def along_z(shift):
                if shift == 0:
                    return centre
                turned = pltpu.roll(centre, (-shift) % cells_z, 1)
                kept = lane_at >= -shift if shift < 0 else lane_at < cells_z - shift
                return jnp.where(kept, turned, 0.0)

            partial[field, y] = (
                2.0 * centre
                - older(field, level, y)
                + medium[0, y] * second(along_x)
                + medium[2, y] * second(along_z)
            )

    def finish(field, level):
        for y in range(slab_y):
            def along_y(shift):
                return levels[level, field, REACH + y + shift, inside, :]

            if field == SRC:
                added = -wavelet[level] * spot[y]
            else:
                added = surface[level, y]
            levels[level + 1, field, REACH + y, inside, :] = (
                partial[field, y] + medium[1, y] * second(along_y) + added
            )

    local(RCV, 0)
    wait_halo(RCV, 0)
    finish(RCV, 0)
    send_halo(RCV, 1)
    local(RCV, 1)

    arrived = landed.at[pl.ds(0, (devices - 1) * block)]
    pltpu.make_async_copy(arrived, arrived, out_recv).wait()
    for y in range(span):
        levels[0, SRC, y, inside, :] = landed[pl.ds(y, cells_x, stride=rows), :]
    local(SRC, 0)
    finish(SRC, 0)
    for level in range(1, steps):
        send_halo(SRC, level)
        local(SRC, level)
        wait_halo(RCV, level)
        finish(RCV, level)
        if level + 1 < steps:
            send_halo(RCV, level + 1)
            local(RCV, level + 1)
        wait_halo(SRC, level)
        finish(SRC, level)

    for back, level in enumerate((steps, steps - 1)):
        for x in range(slab_x):
            for y in range(slab_y):
                at = (back * slab_x + x) * slab_y + y
                leaving[pl.ds(at, devices, stride=back_rows), :] = levels[
                    level, SRC, REACH + y, pl.ds(EDGE + x, devices, stride=slab_x), :
                ]

    def back_copy(peer):
        return pltpu.make_async_remote_copy(
            src_ref=leaving.at[pl.ds(pl.multiple_of(peer * back_rows, 8), back_rows)],
            dst_ref=returned.at[pl.ds(pl.multiple_of(me * back_rows, 8), back_rows)],
            send_sem=back_send,
            recv_sem=back_recv,
            device_id={"wide": peer},
            device_id_type=MESH,
        )

    for distance in far_first:
        back_copy(lax.rem(me + distance, devices)).start()

    own_back = pl.ds(pl.multiple_of(me * back_rows, 8), back_rows)
    returned[own_back, :] = leaving[own_back, :]
    for y in range(slab_y):
        rcv_next[y] = levels[steps, RCV, REACH + y, inside, :]
        rcv_prior[y] = levels[steps - 1, RCV, REACH + y, inside, :]
        for field in (SRC, RCV):
            for snap in range(padded.shape[0]):
                padded[snap, field, y, half : half + cells_x, :] = levels[
                    2 * snap + 2, field, REACH + y, inside, :
                ]
    for plane in range(lags):
        slot = lag_order[plane]
        at_src = pl.ds(2 * half - slot, cells_x)
        at_rcv = pl.ds(slot, cells_x)
        for y in range(slab_y):
            total = None
            for snap in range(padded.shape[0]):
                product = padded[snap, SRC, y, at_src, :] * padded[snap, RCV, y, at_rcv, :]
                total = product if total is None else total + product
            board[plane, y] = total

    sent = staged.at[pl.ds(0, (devices - 1) * block)]
    pltpu.make_async_copy(sent, sent, out_send).wait()
    for level in range(steps):
        wait_sent(RCV, level)
        if level > 0:
            wait_sent(SRC, level)

    came = returned.at[pl.ds(0, (devices - 1) * back_rows)]
    pltpu.make_async_copy(came, came, back_recv).wait()
    for back, result in enumerate((src_next, src_prior)):
        for x in range(slab_x):
            for y in range(slab_y):
                at = (back * slab_x + x) * slab_y + y
                result[x, pl.ds(y, devices, stride=slab_y), :] = returned[
                    pl.ds(at, devices, stride=back_rows), :
                ]
    gone = leaving.at[pl.ds(0, (devices - 1) * back_rows)]
    pltpu.make_async_copy(gone, gone, back_send).wait()


def deliver_kernel(*refs):
    count = (len(refs) - 1) // 2
    planes = refs[count - 1].shape[0]
    cuts = [planes * part // PARTS for part in range(PARTS + 1)]
    pieces = [
        (refs[count - 1].at[pl.ds(low, high - low)], refs[2 * count - 1].at[pl.ds(low, high - low)])
        for low, high in zip(cuts, cuts[1:])
    ]
    pieces += [(refs[i], refs[count + i]) for i in range(count - 1)]
    copies = [
        pltpu.make_async_copy(source, target, refs[-1].at[i])
        for i, (source, target) in enumerate(pieces)
    ]
    for copy in copies:
        copy.start()
    for copy in copies:
        copy.wait()


MESH = pl.DeviceIdType.MESH


def solution(mesh):
    devices = mesh.shape["wide"]

    def on_device(
        src_now, src_old, rcv_now, rcv_old, medium, wavelet, shot, traces, rec_x, lag_order
    ):
        slab_x, cells_y, cells_z = src_now.shape
        slab_y, _, cells_x = rcv_now.shape
        steps = wavelet.shape[0]
        lags = lag_order.shape[0]
        half = (lags - 1) // 2
        span = slab_y + 2 * REACH
        rows = -(-(span + slab_y) // 8) * 8
        f32 = jnp.float32
        vmem = pl.BlockSpec(memory_space=pltpu.VMEM)
        hbm = pl.BlockSpec(memory_space=pltpu.HBM)
        src_shape = jax.ShapeDtypeStruct((slab_x, cells_y, cells_z), f32)
        rcv_shape = jax.ShapeDtypeStruct((slab_y, cells_x, cells_z), f32)
        board_shape = jax.ShapeDtypeStruct((lags, slab_y, cells_x, cells_z), f32)
        shapes = (src_shape, src_shape, rcv_shape, rcv_shape, board_shape)
        taken = steps // 2
        turn = lambda array: jnp.swapaxes(array, -1, -2)
        like = lambda array: pltpu.VMEM(array.shape, array.dtype)
        scalars = lambda array: pltpu.SMEM(array.shape, array.dtype)
        rcv_now, rcv_old, medium, traces = map(turn, (rcv_now, rcv_old, medium, traces))
        scratch = [
            like(src_now),
            like(src_old),
            like(rcv_old),
            like(medium),
            scalars(wavelet),
            scalars(shot),
            like(traces),
            like(rec_x),
            scalars(lag_order),
            pltpu.VMEM((taken, 2, slab_y, cells_x + 2 * half, cells_z), f32),
            pltpu.VMEM((cells_x * rows, cells_z), f32),
            pltpu.VMEM((cells_x * rows, cells_z), f32),
            pltpu.VMEM((steps + 1, 2, span, cells_x + 2 * EDGE, cells_z), f32),
            pltpu.VMEM((2, slab_y, cells_x, cells_z), f32),
            pltpu.VMEM((steps, slab_y, cells_x, cells_z), f32),
            pltpu.VMEM((slab_y, cells_x, cells_z), f32),
            pltpu.VMEM((devices * 2 * slab_x * slab_y, cells_z), f32),
            pltpu.VMEM((devices * 2 * slab_x * slab_y, cells_z), f32),
        ]
        held = sum(4 * math.prod(each.shape) for each in scratch + list(shapes))
        results = pl.pallas_call(
            functools.partial(window_kernel, devices),
            out_shape=shapes,
            in_specs=[hbm] * 10,
            out_specs=(vmem,) * 5,
            scratch_shapes=scratch
            + [pltpu.SemaphoreType.DMA] * 4
            + [
                pltpu.SemaphoreType.DMA((2, steps, 2)),
                pltpu.SemaphoreType.DMA((2, steps, 2)),
                pltpu.SemaphoreType.DMA((10,)),
            ],
            compiler_params=pltpu.CompilerParams(
                collective_id=0, has_side_effects=True, vmem_limit_bytes=held + (4 << 20)
            ),
            name="window",
        )(
            *(
                pltpu.with_memory_space_constraint(array, pltpu.HBM)
                for array in (
                    src_now,
                    src_old,
                    rcv_now,
                    rcv_old,
                    medium,
                    wavelet,
                    shot,
                    traces,
                    rec_x,
                    lag_order,
                )
            )
        )
        outs = pl.pallas_call(
            deliver_kernel,
            out_shape=shapes,
            in_specs=[vmem] * 5,
            out_specs=(hbm,) * 5,
            scratch_shapes=[pltpu.SemaphoreType.DMA((4 + PARTS,))],
            compiler_params=pltpu.CompilerParams(vmem_limit_bytes=held + (4 << 20)),
            name="deliver",
        )(*results)
        return outs[0], outs[1], turn(outs[2]), turn(outs[3]), turn(outs[4])

    return jax.shard_map(
        on_device,
        mesh=mesh,
        in_specs=(
            P("wide", "shots", None),
            P("wide", "shots", None),
            P("wide", "shots", None),
            P("wide", "shots", None),
            P(None, "wide", None, None),
            P(),
            P("shots"),
            P("wide", "shots", None),
            P("wide", "shots"),
            P(),
        ),
        out_specs=(
            P("wide", "shots", None),
            P("wide", "shots", None),
            P("wide", "shots", None),
            P("wide", "shots", None),
            P("shots", "wide", None, None),
        ),
        check_vma=False,
    )
```
